32 devices in a mesh: wide: 16 (over z, y, x), narrow: 2 (over core).
Axes of the slice: x: 2, y: 2, z: 4, core: 2. Of those that a mesh axis runs over, the one named last changes fastest.
Arguments:
- pool_tokens: bfloat16 [12288, 2048], P(('wide', 'narrow')), may hold values from -6 to 6
- cotangent: bfloat16 [24576, 2048], P(('wide', 'narrow')), may hold values from -6 to 6
- slot_weights: bfloat16 [32, 3, 2048, 512], P(('wide', 'narrow')), may hold values from -6 to 6
- row_index: int32 [32, 768], P(('wide', 'narrow')), may hold values from 0 to 383
- route_weight: float32 [32, 768], P(('wide', 'narrow')), may hold values from 0.05 to 1
- slot_expert: int32 [32, 1], replicated, may hold values from 0 to 7
- next_expert: int32 [32, 1], replicated, may hold values from 0 to 7
- master: float32 [8, 3, 2048, 512], P(None, None, ('wide', 'narrow')), may hold values from -6 to 6
- moment_m: float32 [8, 3, 2048, 512], P(None, None, ('wide', 'narrow')), may hold values from -4 to 4
- moment_v: float32 [8, 3, 2048, 512], P(None, None, ('wide', 'narrow')), may hold values from 0.05 to 1
Outputs:
- token_grads: bfloat16 [12288, 2048], P(('wide', 'narrow'))
- master_next: float32 [8, 3, 2048, 512], P(None, None, ('wide', 'narrow'))
- moment_m_next: float32 [8, 3, 2048, 512], P(None, None, ('wide', 'narrow'))
- moment_v_next: float32 [8, 3, 2048, 512], P(None, None, ('wide', 'narrow'))
- next_weights: bfloat16 [32, 3, 2048, 512], P(('wide', 'narrow'))
The draws below stay inside these ranges and needn't reach their ends.
Inputs may be any that keep to these rules, and one draw needn't show every extreme that they name: `slot_expert`: every one of the 8 experts is held by at least one slot; counts are uneven. `next_expert`: every one of the 8 experts is held by at least one slot; counts are uneven. `row_index`: indices into the pool of the slot's own device; a token may appear more than once.
All inputs are finite; a program needn't handle non-finite values.
Results may differ from the reference program's by a relative error of at most 0.0065.
Values may be sent and summed in bfloat16 or wider, within the bound.
A program may use at most 128 MiB of HBM per device.

```python
import math
import jax
import jax.numpy as jnp
from jax import lax

D = 2048
H = 512
EXPERTS = 8
ROWS = 768
POOL = 384
SLOTS = 32
TOKENS = 12288
PACKED = 24576


def place_ends(result, stream_key, least, largest):
    spot = [jax.random.randint(jax.random.fold_in(stream_key, axis), (), 0, length) for axis, length in enumerate(result.shape)]
    longest = result.shape.index(max(result.shape))
    neighbour = spot[:longest] + [(spot[longest] + 1) % result.shape[longest]] + spot[longest + 1:]
    return result.at[tuple(spot)].set(least).at[tuple(neighbour)].set(largest)


def level_of(stream_key, shape, split, least, top_value):
    gain, own = 1.0, jax.random.fold_in(stream_key, 6)
    for position, shards_of in split:
        steps = jnp.exp(jax.random.uniform(jax.random.fold_in(own, position), (shards_of,), jnp.float32, least / len(split), top_value / len(split)))
        gain = gain * jnp.repeat(steps, shape[position] // shards_of).reshape([-1 if axis == position else 1 for axis in range(len(shape))])
    return gain


def different_ones(key, rows, number_of, top, lift):
    sequence = jax.random.permutation(jax.random.fold_in(key, 1), number_of)
    favour = sequence
    for power in range(3):
        favour = favour * favour // number_of
    favour = favour * lift // number_of
    chance = jax.random.randint(jax.random.fold_in(key, 2), (rows, number_of), 0, 4096) + favour
    sure = jax.random.permutation(jax.random.fold_in(key, 3), rows)[jnp.arange(number_of) % rows]
    chance = jnp.where(jnp.arange(rows)[:, None] == sure[None, :], 1 << 14, chance)
    score = chance * number_of + jnp.arange(number_of)
    return lax.top_k(score.astype(jnp.int32), top)[1].astype(jnp.int32)


def normal_values(own_key, shape, spread, bound, pieces=(), kind=jnp.bfloat16):
    drawn = spread * jax.random.normal(own_key, shape, jnp.float32)
    if pieces:
        drawn = drawn * level_of(own_key, shape, pieces, -0.22, 0.18)
    return jnp.clip(drawn, -bound, bound).astype(kind)


def setup_inputs(seed: int = 0) -> dict:
    key_list = jax.random.split(jax.random.key(seed), 11)
    return {
        "pool_tokens": normal_values(key_list[0], (TOKENS, D), 1.0, 6.0, ((0, 32),)),
        "cotangent": normal_values(key_list[1], (PACKED, D), 1.0, 6.0, ((0, 32),)),
        "slot_weights": normal_values(key_list[2], (SLOTS, 3, D, H), 1.0, 6.0, ((0, 32),)),
        "row_index": place_ends(jax.random.randint(key_list[3], (SLOTS, ROWS), 0, POOL), jax.random.fold_in(key_list[3], 1), 0, POOL - 1).astype(jnp.int32),
        "route_weight": jnp.clip(0.05 + 0.95 * jax.random.uniform(key_list[4], (SLOTS, ROWS), jnp.float32) ** level_of(key_list[4], (SLOTS, ROWS), ((0, 32),), -0.2, 0.2), 0.05, 1.0),
        "slot_expert": different_ones(key_list[5], SLOTS, EXPERTS, 1, 2048),
        "next_expert": different_ones(key_list[6], SLOTS, EXPERTS, 1, 2048),
        "master": normal_values(key_list[7], (EXPERTS, 3, D, H), 1.0, 6.0, ((2, 32),), jnp.float32),
        "moment_m": normal_values(key_list[8], (EXPERTS, 3, D, H), 0.3, 4.0, ((2, 32),), jnp.float32),
        "moment_v": jnp.clip(jnp.exp(math.log(1.0) - 2.9957323 * jax.random.uniform(key_list[9], (EXPERTS, 3, D, H), jnp.float32) ** level_of(key_list[9], (EXPERTS, 3, D, H), ((2, 32),), -0.2, 0.2)), 0.05, 1.0),
    }


def inner(left, right):
    return lax.dot_general(left, right, (((0,), (0,)), ((), ())), preferred_element_type=jnp.float32)

def against(left, right):
    return lax.dot_general(left, right, (((1,), (1,)), ((), ())), preferred_element_type=jnp.float32)

def slot_pass(rows, cotangent, weights, route):
    scale_in = weights.shape[1] ** (-0.5)
    scale_out = weights.shape[2] ** (-0.5)
    gate = jnp.dot(rows, weights[0], preferred_element_type=jnp.float32) * scale_in
    upper = jnp.dot(rows, weights[1], preferred_element_type=jnp.float32) * scale_in
    sigma = jax.nn.sigmoid(gate)
    active = gate * sigma
    hidden = (active * upper).astype(jnp.bfloat16)
    scaled = (route[:, None] * cotangent.astype(jnp.float32)).astype(jnp.bfloat16)
    back = jnp.dot(scaled, weights[2], preferred_element_type=jnp.float32) * scale_out
    d_gate = (back * upper * sigma * (1.0 + gate * (1.0 - sigma))).astype(jnp.bfloat16)
    d_up = (back * active).astype(jnp.bfloat16)
    grads = jnp.stack([inner(rows, d_gate) * scale_in, inner(rows, d_up) * scale_in, inner(scaled, hidden) * scale_out])
    inputs = (against(d_gate, weights[0]) + against(d_up, weights[1])) * scale_in
    return (grads, inputs)

def adam_step(grad, master, moment_m, moment_v):
    first = 0.9 * moment_m + 0.1 * grad
    second = 0.95 * moment_v + 0.05 * grad * grad
    fresh = master - 0.05 * (first / (jnp.sqrt(second) + 1e-08) + 0.1 * master)
    return (fresh, first, second)

def reference(pool_tokens, cotangent, slot_weights, row_index, route_weight, slot_expert, next_expert, master, moment_m, moment_v):
    pools = pool_tokens.reshape(SLOTS, POOL, D)
    cots = cotangent.reshape(SLOTS, ROWS, D)

    def visit(total, item):
        pool, cot, weights, index, route, expert = item
        rows = jnp.take(pool, index, axis=0)
        grads, inputs = slot_pass(rows, cot, weights, route)
        total = total.at[expert].add(grads)
        grad_pool = jnp.zeros((POOL, D), jnp.float32).at[index].add(inputs).astype(jnp.bfloat16)
        return (total, grad_pool)
    start = jnp.zeros((EXPERTS, 3, D, H), jnp.float32)
    total, grad_pools = lax.scan(visit, start, (pools, cots, slot_weights, row_index, route_weight, slot_expert[:, 0]))
    fresh, first, second = adam_step(total, master, moment_m, moment_v)
    next_weights = jnp.take(fresh.astype(jnp.bfloat16), next_expert[:, 0], axis=0)
    return (grad_pools.reshape(TOKENS, D), fresh, first, second, next_weights)
```

```python
import functools

import jax
import jax.numpy as jnp
from jax import lax
from jax.experimental import pallas as pl
from jax.experimental.pallas import tpu as pltpu
from jax.sharding import PartitionSpec as P

MESH = pl.DeviceIdType.MESH
LAYERS = 4
CHUNK_COLS = 128
UNIT = 2
ROW_TILE = 16
WIDE_TILE = 512
LONG_TILE = 384
UNROLL = 8
SPLIT = 2
AHEAD = 4
ORDER = (
    ("ends", -1),
    ("mids", 0, 0),
    ("relay", 4, 3),
    ("relay", 3, 2),
    ("relay", 2, 1),
    ("update", 1),
    ("mids", 0, 1),
    ("mids", 0, 2),
)


def inner(left, right):
    return lax.dot_general(
        left, right, (((0,), (0,)), ((), ())), preferred_element_type=jnp.float32
    )


def against(left, right):
    return lax.dot_general(
        left, right, (((1,), (1,)), ((), ())), preferred_element_type=jnp.float32
    )


def drain(ref, sem):
    pltpu.make_async_copy(ref, ref, sem).wait()


def exchange(
    narrow_count,
    members,
    experts_now,
    nexts,
    row_index,
    route,
    pool,
    cotangent,
    weights,
    master,
    moment_m,
    moment_v,
    master_out,
    m_out,
    v_out,
    next_out,
    tokens_out,
    owners,
    made,
    acts,
    rights,
    spread,
    route_column,
    gates,
    w_held,
    token_sums,
    recv,
    inbox,
    shelf,
    in_sem,
    load_sem,
    own_sem,
    a2a_send,
    a2a_recv,
    part_send,
    part_recv,
    fresh_send,
    fresh_recv,
    out_send,
    out_recv,
):
    experts, parts, block, hidden_units = master_out.shape
    chunks, plane, layers, piece_rows, cols = made.shape
    split = block // piece_rows
    group = UNIT * split
    per_part = hidden_units // cols * split
    width = w_held.shape[1]
    length = acts.shape[1]
    scale_in = width ** (-0.5)
    scale_out = hidden_units ** (-0.5)
    states = (master_out, m_out, v_out)
    last = layers - 1
    me = lax.axis_index("wide") * narrow_count + lax.axis_index("narrow")
    layer = me // plane
    spot = me % plane
    base = layer * plane
    has_below = layer > 0
    has_above = layer < last

    def device(index):
        return (index // narrow_count, index % narrow_count)

    def peer_of(step):
        return (spot + step) % plane

    def part_of(ch):
        return (ch // per_part + parts - 1) % parts

    def cols_of(ch):
        return pl.ds(pl.multiple_of((ch % per_part) // split * cols, cols), cols)

    def rows_of(ch, start=0, size=piece_rows):
        first = (ch % split) * piece_rows + start
        return pl.ds(pl.multiple_of(first, size), size)

    barrier = pltpu.get_barrier_semaphore()

    def hello(index):
        pl.semaphore_signal(barrier, inc=1, device_id=device(index), device_id_type=MESH)

    def greet(step, carry):
        hello(base + peer_of(step))
        return carry

    lax.fori_loop(1, plane, greet, 0)

    @pl.when(has_below)
    def _():
        hello(me - plane)

    @pl.when(has_above)
    def _():
        hello(me + plane)

    def meet():
        beside = has_below.astype(jnp.int32) + has_above.astype(jnp.int32)
        pl.semaphore_wait(barrier, plane - 1 + beside)

    def tiles_of(size, most, body):
        tile = min(most, size)

        def step(t, carry):
            body(pl.ds(pl.multiple_of(t * tile, tile), tile))
            return carry

        lax.fori_loop(0, size // tile, step, 0)

    def wide_tiles(body):
        tiles_of(width, WIDE_TILE, body)

    def long_tiles(body):
        tiles_of(length, LONG_TILE, body)

    def product_of(left, right):
        return jnp.dot(left, right, preferred_element_type=jnp.float32)

    def pick_rows():
        tokens = lax.broadcasted_iota(jnp.int32, spread.shape, 0)
        spread[...] = jnp.where(tokens == row_index[...], 1.0, 0.0).astype(jnp.bfloat16)
        route_column[...] = jnp.transpose(jnp.broadcast_to(route[...], (128, length)))

    def gather(span):
        acts[0, :, span] = inner(spread[...], tokens_out[:, span]).astype(jnp.bfloat16)

    def forward(span):
        rows = acts[0, span, :]
        gate = product_of(rows, w_held[0]) * scale_in
        upper = product_of(rows, w_held[1]) * scale_in
        gates[0, span, :] = gate
        gates[1, span, :] = upper
        rights[parts - 1, span, :] = (gate * jax.nn.sigmoid(gate) * upper).astype(jnp.bfloat16)

    def scale_rows(span):
        column = route_column[span, pl.ds(0, 1)]
        acts[1, span, :] = (column * acts[1, span, :].astype(jnp.float32)).astype(jnp.bfloat16)

    def backward(span):
        back = product_of(acts[1, span, :], w_held[2]) * scale_out
        gate = gates[0, span, :]
        upper = gates[1, span, :]
        sigma = jax.nn.sigmoid(gate)
        slope = sigma * (1.0 + gate * (1.0 - sigma))
        rights[0, span, :] = (back * upper * slope).astype(jnp.bfloat16)
        rights[1, span, :] = (back * (gate * sigma)).astype(jnp.bfloat16)

    def make(unit):
        ch = unit * group
        k = part_of(ch)
        side = jnp.where(k == parts - 1, 1, 0)
        scale = jnp.where(k == parts - 1, scale_out, scale_in).astype(jnp.float32)
        start = pl.multiple_of((ch % per_part) // split * cols, UNIT * cols)

        def of_layer(l, carry):
            span = pl.ds(pl.multiple_of(l * (plane * block), plane * block), plane * block)
            right = rights[k, :, pl.ds(start, UNIT * cols)]
            product = (inner(acts[side, :, span], right) * scale).astype(jnp.bfloat16)
            for j in range(UNIT):
                piece = product[:, j * cols : (j + 1) * cols]
                piece = piece.reshape(plane, split, piece_rows, cols)
                for r in range(split):
                    made[ch + j * split + r, :, l] = piece[:, r]
            return carry

        lax.fori_loop(0, layers, of_layer, 0)

    def scatter(ch):
        def send(step, carry):
            peer = peer_of(step)
            pltpu.make_async_remote_copy(
                src_ref=made.at[ch, peer],
                dst_ref=recv.at[ch, spot],
                send_sem=a2a_send.at[ch],
                recv_sem=a2a_recv.at[ch],
                device_id=device(base + peer),
                device_id_type=MESH,
            ).start()
            return carry

        lax.fori_loop(1, plane, send, 0)
        pltpu.make_async_copy(made.at[ch, spot], recv.at[ch, spot], own_sem.at[ch]).start()

    def collect(ch):
        drain(recv.at[ch, pl.ds(0, plane - 1)], a2a_recv.at[ch])
        drain(recv.at[ch, 0], own_sem.at[ch])

    def tabulate(s, carry):
        for e in range(experts):
            owners[e * plane + s] = jnp.where(experts_now[base + s] == e, 1.0, 0.0)
        return carry

    row_tile = min(ROW_TILE, piece_rows)

    def row_tiles(body):
        def step(t, carry):
            body(pl.multiple_of(t * row_tile, row_tile))
            return carry

        lax.fori_loop(0, piece_rows // row_tile, step, 0)

    def sums(ch, l, rows, init):
        def add(outer, totals):
            for u in range(UNROLL):
                s = outer * UNROLL + u
                value = recv[ch, s, l, rows, :].astype(jnp.float32)
                totals = tuple(
                    total + value * owners[e * plane + s] for e, total in enumerate(totals)
                )
            return totals

        return lax.fori_loop(0, plane // UNROLL, add, init)

    def pass_on(ch, q):
        low = layer * 2 < layers
        ups = last - layer
        up = jnp.where(low, q < ups, q >= layer)
        l = jnp.where(
            low,
            jnp.where(q < ups, last - q, q - ups),
            jnp.where(q < layer, q, last - (q - layer)),
        )
        fed = jnp.where(up, has_below, has_above)
        target = jnp.where(up, me + plane, me - plane)
        place = jnp.where(up, l, jnp.where(l == layer - 1, layers, l))

        @pl.when(fed)
        def _():
            drain(inbox.at[0, 0], part_recv.at[ch, l])

        def body(start):
            rows = pl.ds(start, row_tile)
            init = tuple(inbox[ch, l, e, rows, :].astype(jnp.float32) for e in range(experts))
            totals = sums(ch, l, rows, init)
            for e, total in enumerate(totals):
                recv[ch, e, l, rows, :] = total.astype(jnp.bfloat16)

        row_tiles(body)
        pltpu.make_async_remote_copy(
            src_ref=recv.at[ch, pl.ds(0, experts), l],
            dst_ref=inbox.at[ch, place],
            send_sem=part_send,
            recv_sem=part_recv.at[ch, place],
            device_id=device(target),
            device_id_type=MESH,
        ).start()

    def hand(ch, l, target):
        pltpu.make_async_remote_copy(
            src_ref=inbox.at[ch, l],
            dst_ref=inbox.at[ch, l],
            send_sem=fresh_send,
            recv_sem=fresh_recv.at[ch, l],
            device_id=device(target),
            device_id_type=MESH,
        ).start()

    def refill(ch, l):
        k = part_of(ch)
        owner = l * plane + spot
        span = cols_of(ch)
        rows = rows_of(ch)

        def fill(step, carry):
            peer = peer_of(step)
            made[ch, peer, l] = shelf[nexts[base + peer]]
            pltpu.make_async_remote_copy(
                src_ref=made.at[ch, peer, l],
                dst_ref=next_out.at[k, owner, rows, span],
                send_sem=out_send,
                recv_sem=out_recv,
                device_id=device(base + peer),
                device_id_type=MESH,
            ).start()
            return carry

        shelf[...] = inbox[ch, l]
        lax.fori_loop(1, plane, fill, 0)
        next_out[k, owner, rows, span] = shelf[nexts[me]]

    def update(ch):
        k = part_of(ch)
        span = cols_of(ch)

        @pl.when(has_below)
        def _():
            drain(inbox.at[0, 0], part_recv.at[ch, layer])

        @pl.when(has_above)
        def _():
            drain(inbox.at[0, 0], part_recv.at[ch, layers])

        def body(start):
            rows = pl.ds(start, row_tile)
            state_rows = rows_of(ch, start, row_tile)
            init = tuple(
                inbox[ch, layer, e, rows, :].astype(jnp.float32)
                + inbox[ch, layers, e, rows, :].astype(jnp.float32)
                for e in range(experts)
            )
            totals = sums(ch, layer, rows, init)
            for e, grad in enumerate(totals):
                held = states[0][e, k, state_rows, span]
                first = 0.9 * states[1][e, k, state_rows, span] + 0.1 * grad
                second = 0.95 * states[2][e, k, state_rows, span] + 0.05 * grad * grad
                value = held - 0.05 * (first / (jnp.sqrt(second) + 1e-08) + 0.1 * held)
                states[0][e, k, state_rows, span] = value
                states[1][e, k, state_rows, span] = first
                states[2][e, k, state_rows, span] = second
                inbox[ch, layer, e, rows, :] = value.astype(jnp.bfloat16)

        row_tiles(body)

        @pl.when(has_above)
        def _():
            hand(ch, layer, me + plane)

        @pl.when(has_below)
        def _():
            hand(ch, layer, me - plane)

        drain(recv.at[ch, pl.ds(0, plane - 1)], a2a_send.at[ch])
        refill(ch, layer)

    def relay(ch, hop):
        below = layer - hop
        above = layer + hop

        @pl.when(below >= 0)
        def _():
            drain(inbox.at[0, 0], fresh_recv.at[ch, below])

            @pl.when(has_above)
            def _():
                hand(ch, below, me + plane)

        @pl.when(above <= last)
        def _():
            drain(inbox.at[0, 0], fresh_recv.at[ch, above])

            @pl.when(has_below)
            def _():
                hand(ch, above, me - plane)

        @pl.when(below >= 0)
        def _():
            refill(ch, below)

        @pl.when(above <= last)
        def _():
            refill(ch, above)

    def loads():
        for i, ref in enumerate((master, moment_m, moment_v)):
            pltpu.make_async_copy(ref, states[i], load_sem.at[i]).start()

    def clear():
        zero = jnp.zeros((experts, piece_rows, cols), jnp.bfloat16)

        @pl.when(layer == 0)
        def _():
            def wipe(t, carry):
                inbox[t // layers, t % layers] = zero
                return carry

            lax.fori_loop(0, chunks * layers, wipe, 0)

        @pl.when(layer == last)
        def _():
            def wipe(t, carry):
                inbox[t // layers, jnp.where(t % layers == last, layers, t % layers)] = zero
                return carry

            lax.fori_loop(0, chunks * layers, wipe, 0)

    def token_grads(piece):
        @pl.when(piece == 0)
        def _():
            for k in range(parts - 1):
                token_sums[k] = product_of(spread[...], rights[k]).astype(jnp.bfloat16)

        tile = min(WIDE_TILE, width)

        @pl.when((piece >= 0) & (piece < width // tile))
        def _():
            span = pl.ds(pl.multiple_of(piece * tile, tile), tile)
            total = against(token_sums[0], w_held[0, span, :])
            total = total + against(token_sums[1], w_held[1, span, :])
            tokens_out[:, span] = (total * scale_in).astype(jnp.bfloat16)

    inputs = ((pool, tokens_out), (weights.at[0], w_held), (cotangent, acts.at[1]))
    arrivals = [
        pltpu.make_async_copy(src, dst, in_sem.at[i]) for i, (src, dst) in enumerate(inputs)
    ]
    for arrival in arrivals:
        arrival.start()
    pick_rows()
    clear()
    lax.fori_loop(0, plane, tabulate, 0)
    arrivals[0].wait()
    wide_tiles(gather)
    arrivals[1].wait()
    long_tiles(forward)
    arrivals[2].wait()
    long_tiles(scale_rows)
    meet()

    def produce(unit, carry):
        make(unit)
        for j in range(group):
            scatter(unit * group + j)
        return carry

    produce(0, 0)
    loads()
    lax.fori_loop(1, AHEAD // UNIT, produce, 0)
    long_tiles(backward)
    for i in range(3):
        drain(states[i], load_sem.at[i])
    is_end = (layer == 0) | (layer == last)
    ahead = AHEAD * split

    def perform(i, op, lag, *extra):
        ch = i - lag
        valid = (ch >= 0) & (ch < chunks)
        if op == "ends":

            @pl.when(valid & is_end)
            def _():
                collect(ch)

                def one(q, carry):
                    pass_on(ch, q)
                    return carry

                lax.fori_loop(0, last, one, 0)

        if op == "mids":

            @pl.when(valid & jnp.logical_not(is_end))
            def _():
                if extra[0] == 0:
                    collect(ch)
                pass_on(ch, extra[0])

        if op == "update":

            @pl.when(valid)
            def _():
                update(ch)

        if op == "relay":

            @pl.when(valid)
            def _():
                relay(ch, extra[0])

    def body(i, carry):
        @pl.when((i >= 0) & (i % group == 0) & (i + ahead < chunks))
        def _():
            produce((i + ahead) // group, 0)

        for step in ORDER:
            perform(i, *step)
        token_grads(i - (chunks - ahead))
        return carry

    lags = [step[1] for step in ORDER]
    lax.fori_loop(min(lags), chunks + max(lags), body, 0)

    def finish(ch, carry):
        drain(inbox.at[ch, pl.ds(0, layers - 1)], part_send)
        drain(inbox.at[ch, 0], fresh_send)

        @pl.when(has_below & has_above)
        def _():
            drain(inbox.at[ch, pl.ds(0, layers)], fresh_send)

        return carry

    lax.fori_loop(0, chunks, finish, 0)
    for _ in range(layers):
        drain(next_out.at[:, pl.ds(0, plane - 1)], out_send)
    drain(next_out.at[:, pl.ds(0, (plane - 1) * layers)], out_recv)


def local(
    pool_tokens,
    cotangent,
    slot_weights,
    row_index,
    route_weight,
    slot_expert,
    next_expert,
    master,
    moment_m,
    moment_v,
):
    narrow_count = lax.axis_size("narrow")
    members = lax.axis_size("wide") * narrow_count
    parts, width, hidden_units = slot_weights.shape[1:]
    experts = master.shape[0]
    block = width // members
    length = row_index.shape[1]
    pool_count = pool_tokens.shape[0]
    plane = members // LAYERS
    cols = CHUNK_COLS
    split = min(SPLIT, max(1, block // ROW_TILE))
    piece = block // split
    chunks = parts * (hidden_units // cols) * split
    anywhere = pl.BlockSpec(memory_space=pl.ANY)
    scalars = pl.BlockSpec(memory_space=pltpu.SMEM)
    dma = pltpu.SemaphoreType.DMA
    bf16 = jnp.bfloat16
    state = pltpu.VMEM(master.shape, jnp.float32)
    held = pl.BlockSpec(memory_space=pltpu.VMEM)
    fresh, first, second, refilled, token_grads = pl.pallas_call(
        functools.partial(exchange, narrow_count, members),
        out_shape=(
            state,
            state,
            state,
            pltpu.VMEM((parts, members, block, hidden_units), bf16),
            pltpu.VMEM(pool_tokens.shape, bf16),
        ),
        in_specs=[scalars, scalars, held, held] + [anywhere] * 6,
        out_specs=(held,) * 5,
        scratch_shapes=[
            pltpu.SMEM((experts * plane,), jnp.float32),
            pltpu.VMEM((chunks, plane, LAYERS, piece, cols), bf16),
            pltpu.VMEM((2, length, width), bf16),
            pltpu.VMEM((parts, length, hidden_units), bf16),
            pltpu.VMEM((pool_count, length), bf16),
            pltpu.VMEM((length, 128), jnp.float32),
            pltpu.VMEM((2, length, hidden_units), jnp.float32),
            pltpu.VMEM((parts, width, hidden_units), bf16),
            pltpu.VMEM((2, pool_count, hidden_units), bf16),
            pltpu.VMEM((chunks, plane, LAYERS, piece, cols), bf16),
            pltpu.VMEM((chunks, LAYERS + 1, experts, piece, cols), bf16),
            pltpu.VMEM((experts, piece, cols), bf16),
            dma((3,)),
            dma((3,)),
            dma((chunks,)),
            dma((chunks,)),
            dma((chunks,)),
            dma,
            dma((chunks, LAYERS + 1)),
            dma,
            dma((chunks, LAYERS)),
            dma,
            dma,
        ],
        compiler_params=pltpu.CompilerParams(
            collective_id=0, has_side_effects=True, vmem_limit_bytes=46 * 1024 * 1024
        ),
    )(
        slot_expert[:, 0],
        next_expert[:, 0],
        row_index,
        route_weight,
        pool_tokens,
        cotangent,
        slot_weights,
        master,
        moment_m,
        moment_v,
    )
    next_weights = refilled.reshape(1, parts, width, hidden_units)
    return (token_grads, fresh, first, second, next_weights)


def solution(mesh):
    in_specs = (
        P(("wide", "narrow"), None),
        P(("wide", "narrow"), None),
        P(("wide", "narrow"), None, None, None),
        P(("wide", "narrow"), None),
        P(("wide", "narrow"), None),
        P(),
        P(),
        P(None, None, ("wide", "narrow"), None),
        P(None, None, ("wide", "narrow"), None),
        P(None, None, ("wide", "narrow"), None),
    )
    out_specs = (
        P(("wide", "narrow"), None),
        P(None, None, ("wide", "narrow"), None),
        P(None, None, ("wide", "narrow"), None),
        P(None, None, ("wide", "narrow"), None),
        P(("wide", "narrow"), None, None, None),
    )
    return jax.shard_map(local, mesh=mesh, in_specs=in_specs, out_specs=out_specs, check_vma=False)
```

```python
import functools

import jax
import jax.numpy as jnp
from jax import lax
from jax.experimental import pallas as pl
from jax.experimental.pallas import tpu as pltpu
from jax.sharding import PartitionSpec as P

MESH = pl.DeviceIdType.MESH
LAYERS = 4
CHUNK_COLS = 128
UNIT = 2
ROW_TILE = 16
WIDE_TILE = 512
LONG_TILE = 384
UNROLL = 8
SPLIT = 2
START = 1
ORDER = (
    ("ends", -1),
    ("mids", 0, 0),
    ("relay", 4, 3),
    ("relay", 3, 2),
    ("relay", 2, 1),
    ("update", 1),
    ("mids", 0, 2),
    ("mids", 0, 1),
    ("refill", 4),
)


def inner(left, right):
    return lax.dot_general(
        left, right, (((0,), (0,)), ((), ())), preferred_element_type=jnp.float32
    )


def against(left, right):
    return lax.dot_general(
        left, right, (((1,), (1,)), ((), ())), preferred_element_type=jnp.float32
    )


def drain(ref, sem):
    pltpu.make_async_copy(ref, ref, sem).wait()


def exchange(
    narrow_count,
    members,
    experts_now,
    nexts,
    row_index,
    route,
    pool,
    cotangent,
    weights,
    master,
    moment_m,
    moment_v,
    master_out,
    m_out,
    v_out,
    next_out,
    tokens_out,
    owners,
    made,
    pool_twice,
    scaled,
    hidden,
    d_held,
    spread,
    route_column,
    gates,
    w_held,
    token_sums,
    recv,
    inbox,
    shelf,
    in_sem,
    load_sem,
    own_sem,
    a2a_send,
    a2a_recv,
    part_send,
    part_recv,
    fresh_send,
    fresh_recv,
    out_send,
    out_recv,
):
    experts, parts, block, hidden_units = master_out.shape
    chunks, plane, layers, piece_rows, cols = made.shape
    split = block // piece_rows
    group = UNIT * split
    per_part = hidden_units // cols * split
    width = w_held.shape[1]
    length = scaled.shape[0]
    pool_count = tokens_out.shape[0]
    scale_in = width ** (-0.5)
    scale_out = hidden_units ** (-0.5)
    states = (master_out, m_out, v_out)
    last = layers - 1
    me = lax.axis_index("wide") * narrow_count + lax.axis_index("narrow")
    layer = me // plane
    spot = me % plane
    base = layer * plane
    has_below = layer > 0
    has_above = layer < last

    def device(index):
        return (index // narrow_count, index % narrow_count)

    def peer_of(step):
        peer = spot + step
        return jnp.where(peer >= plane, peer - plane, peer)

    def others(body):
        if plane <= UNROLL:
            for step in range(1, plane):
                body(peer_of(step))
        else:

            def one(step, carry):
                body(peer_of(step))
                return carry

            lax.fori_loop(1, plane, one, 0)

    def part_of(ch):
        return (ch // per_part + parts - 1) % parts

    def cols_of(ch):
        return pl.ds(pl.multiple_of((ch % per_part) // split * cols, cols), cols)

    def rows_of(ch, start=0, size=piece_rows):
        first = (ch % split) * piece_rows + start
        return pl.ds(pl.multiple_of(first, size), size)

    barrier = pltpu.get_barrier_semaphore()

    def hello(index):
        pl.semaphore_signal(barrier, inc=1, device_id=device(index), device_id_type=MESH)

    others(lambda peer: hello(base + peer))

    @pl.when(has_below)
    def _():
        hello(me - plane)

    @pl.when(has_above)
    def _():
        hello(me + plane)

    def meet():
        beside = has_below.astype(jnp.int32) + has_above.astype(jnp.int32)
        pl.semaphore_wait(barrier, plane - 1 + beside)

    def tiles_of(size, most, body):
        tile = min(most, size)

        def step(t, carry):
            body(pl.ds(pl.multiple_of(t * tile, tile), tile))
            return carry

        lax.fori_loop(0, size // tile, step, 0)

    def wide_tiles(body):
        tiles_of(width, WIDE_TILE, body)

    def long_tiles(body):
        tiles_of(length, LONG_TILE, body)

    def product_of(left, right):
        return jnp.dot(left, right, preferred_element_type=jnp.float32)

    def pick_rows():
        tokens = lax.broadcasted_iota(jnp.int32, spread.shape, 0)
        spread[...] = jnp.where(tokens == row_index[...], 1.0, 0.0).astype(jnp.bfloat16)
        route_column[...] = jnp.transpose(jnp.broadcast_to(route[...], (128, length)))

    def forward(h):
        span = pl.ds(pl.multiple_of(h * (UNIT * cols), UNIT * cols), UNIT * cols)
        for j in range(parts - 1):
            value = product_of(pool_twice[pl.ds(0, pool_count), :], w_held[j, :, span]) * scale_in
            high = value.astype(jnp.bfloat16)
            low = (value - high.astype(jnp.float32)).astype(jnp.bfloat16)
            gates[j, :, span] = inner(spread[...], high) + inner(spread[...], low)

        def finish_rows(rows):
            gate = gates[0, rows, span]
            upper = gates[1, rows, span]
            hidden[rows, span] = (gate * jax.nn.sigmoid(gate) * upper).astype(jnp.bfloat16)

        long_tiles(finish_rows)

    def scale_rows(span):
        column = route_column[span, pl.ds(0, 1)]
        scaled[span, :] = (column * scaled[span, :].astype(jnp.float32)).astype(jnp.bfloat16)

    def backward(span):
        back = product_of(scaled[span, :], w_held[2]) * scale_out
        gate = gates[0, span, :]
        upper = gates[1, span, :]
        sigma = jax.nn.sigmoid(gate)
        slope = sigma * (1.0 + gate * (1.0 - sigma))
        d_held[0, span, :] = (back * upper * slope).astype(jnp.bfloat16)
        d_held[1, span, :] = (back * (gate * sigma)).astype(jnp.bfloat16)

    def sum_tokens():
        for k in range(parts - 1):
            value = product_of(spread[...], d_held[k])
            high = value.astype(jnp.bfloat16)
            token_sums[k, pl.ds(0, pool_count), :] = high
            low = value - high.astype(jnp.float32)
            token_sums[k, pl.ds(pool_count, pool_count), :] = low.astype(jnp.bfloat16)

    def make(unit, first, count):
        ch = unit * group
        k = part_of(ch)
        start = pl.multiple_of((ch % per_part) // split * cols, UNIT * cols)
        right_span = pl.ds(start, UNIT * cols)

        def of_layer(l, left, right, scale):
            product = (inner(left, right) * scale).astype(jnp.bfloat16)
            for j in range(UNIT):
                piece = product[:, j * cols : (j + 1) * cols]
                piece = piece.reshape(plane, split, piece_rows, cols)
                for r in range(split):
                    made[ch + j * split + r, :, l] = piece[:, r]

        def span_of(l):
            return pl.ds(pl.multiple_of(l * (plane * block), plane * block), plane * block)

        @pl.when(k == parts - 1)
        def _():
            def down(l, carry):
                of_layer(l, scaled[:, span_of(l)], hidden[:, right_span], scale_out)
                return carry

            lax.fori_loop(first, first + count, down, 0)

        @pl.when(k != parts - 1)
        def _():
            def into(l, carry):
                of_layer(l, pool_twice[:, span_of(l)], token_sums[k, :, right_span], scale_in)
                return carry

            lax.fori_loop(first, first + count, into, 0)

    def scatter(ch):
        def send(peer):
            pltpu.make_async_remote_copy(
                src_ref=made.at[ch, peer],
                dst_ref=recv.at[ch, spot],
                send_sem=a2a_send.at[ch],
                recv_sem=a2a_recv.at[ch],
                device_id=device(base + peer),
                device_id_type=MESH,
            ).start()

        others(send)
        pltpu.make_async_copy(made.at[ch, spot], recv.at[ch, spot], own_sem.at[ch]).start()

    def collect(ch):
        drain(recv.at[ch, pl.ds(0, plane - 1)], a2a_recv.at[ch])
        drain(recv.at[ch, 0], own_sem.at[ch])

    def tabulate(s, carry):
        for e in range(experts):
            owners[e * plane + s] = jnp.where(experts_now[base + s] == e, 1.0, 0.0)
        return carry

    row_tile = min(ROW_TILE, piece_rows)

    def row_tiles(body):
        def step(t, carry):
            body(pl.multiple_of(t * row_tile, row_tile))
            return carry

        lax.fori_loop(0, piece_rows // row_tile, step, 0)

    def sums(ch, l, rows, init):
        def add(outer, totals):
            for u in range(UNROLL):
                s = outer * UNROLL + u
                value = recv[ch, s, l, rows, :].astype(jnp.float32)
                totals = tuple(
                    total + value * owners[e * plane + s] for e, total in enumerate(totals)
                )
            return totals

        return lax.fori_loop(0, plane // UNROLL, add, init)

    def pass_on(ch, q):
        low = layer * 2 < layers
        ups = last - layer
        up = jnp.where(low, q < ups, q >= layer)
        l = jnp.where(
            low,
            jnp.where(q < ups, last - q, q - ups),
            jnp.where(q < layer, q, last - (q - layer)),
        )
        fed = jnp.where(up, has_below, has_above)
        target = jnp.where(up, me + plane, me - plane)
        place = jnp.where(up, l, jnp.where(l == layer - 1, layers, l))

        @pl.when(fed)
        def _():
            drain(inbox.at[0, 0], part_recv.at[ch, l])

        def body(start):
            rows = pl.ds(start, row_tile)
            init = tuple(inbox[ch, l, e, rows, :].astype(jnp.float32) for e in range(experts))
            totals = sums(ch, l, rows, init)
            for e, total in enumerate(totals):
                recv[ch, e, l, rows, :] = total.astype(jnp.bfloat16)

        row_tiles(body)
        pltpu.make_async_remote_copy(
            src_ref=recv.at[ch, pl.ds(0, experts), l],
            dst_ref=inbox.at[ch, place],
            send_sem=part_send,
            recv_sem=part_recv.at[ch, place],
            device_id=device(target),
            device_id_type=MESH,
        ).start()

    def hand(ch, l, target):
        pltpu.make_async_remote_copy(
            src_ref=inbox.at[ch, l],
            dst_ref=inbox.at[ch, l],
            send_sem=fresh_send,
            recv_sem=fresh_recv.at[ch, l],
            device_id=device(target),
            device_id_type=MESH,
        ).start()

    def refill(ch):
        k = part_of(ch)
        span = cols_of(ch)
        rows = rows_of(ch)
        drain(recv.at[ch, pl.ds(0, plane - 1)], a2a_send.at[ch])
        for l in range(layers):
            shelf[l] = inbox[ch, l]

        def fill(peer):
            which = nexts[base + peer]
            for l in range(layers):
                made[ch, peer, l] = shelf[l, which]
            pltpu.make_async_remote_copy(
                src_ref=made.at[ch, peer],
                dst_ref=next_out.at[k, :, spot, rows, span],
                send_sem=out_send,
                recv_sem=out_recv,
                device_id=device(base + peer),
                device_id_type=MESH,
            ).start()

        others(fill)
        which = nexts[me]
        for l in range(layers):
            next_out[k, l, spot, rows, span] = shelf[l, which]

    def update(ch):
        k = part_of(ch)
        span = cols_of(ch)

        @pl.when(has_below)
        def _():
            drain(inbox.at[0, 0], part_recv.at[ch, layer])

        @pl.when(has_above)
        def _():
            drain(inbox.at[0, 0], part_recv.at[ch, layers])

        def body(start):
            rows = pl.ds(start, row_tile)
            state_rows = rows_of(ch, start, row_tile)
            init = tuple(
                inbox[ch, layer, e, rows, :].astype(jnp.float32)
                + inbox[ch, layers, e, rows, :].astype(jnp.float32)
                for e in range(experts)
            )
            totals = sums(ch, layer, rows, init)
            for e, grad in enumerate(totals):
                held = states[0][e, k, state_rows, span]
                first = 0.9 * states[1][e, k, state_rows, span] + 0.1 * grad
                second = 0.95 * states[2][e, k, state_rows, span] + 0.05 * grad * grad
                value = held - 0.05 * (first / (jnp.sqrt(second) + 1e-08) + 0.1 * held)
                states[0][e, k, state_rows, span] = value
                states[1][e, k, state_rows, span] = first
                states[2][e, k, state_rows, span] = second
                inbox[ch, layer, e, rows, :] = value.astype(jnp.bfloat16)

        row_tiles(body)

        @pl.when(has_above)
        def _():
            hand(ch, layer, me + plane)

        @pl.when(has_below)
        def _():
            hand(ch, layer, me - plane)


    def relay(ch, hop):
        below = layer - hop
        above = layer + hop

        @pl.when(below >= 0)
        def _():
            drain(inbox.at[0, 0], fresh_recv.at[ch, below])

            @pl.when(has_above)
            def _():
                hand(ch, below, me + plane)

        @pl.when(above <= last)
        def _():
            drain(inbox.at[0, 0], fresh_recv.at[ch, above])

            @pl.when(has_below)
            def _():
                hand(ch, above, me - plane)

    def loads():
        for i, ref in enumerate((master, moment_m, moment_v)):
            pltpu.make_async_copy(ref, states[i], load_sem.at[i]).start()

    def clear():
        zero = jnp.zeros((experts, piece_rows, cols), jnp.bfloat16)

        @pl.when(layer == 0)
        def _():
            def wipe(t, carry):
                inbox[t // layers, t % layers] = zero
                return carry

            lax.fori_loop(0, chunks * layers, wipe, 0)

        @pl.when(layer == last)
        def _():
            def wipe(t, carry):
                inbox[t // layers, jnp.where(t % layers == last, layers, t % layers)] = zero
                return carry

            lax.fori_loop(0, chunks * layers, wipe, 0)

    def token_grads(piece):
        tile = min(WIDE_TILE, width)

        @pl.when((piece >= 0) & (piece < width // tile))
        def _():
            span = pl.ds(pl.multiple_of(piece * tile, tile), tile)
            total = against(token_sums[0, pl.ds(0, pool_count), :], w_held[0, span, :])
            total = total + against(token_sums[1, pl.ds(0, pool_count), :], w_held[1, span, :])
            tokens_out[:, span] = (total * scale_in).astype(jnp.bfloat16)

    halves = hidden_units // (UNIT * cols)

    def half_of(h):
        span = pl.ds(h * (UNIT * cols), UNIT * cols)
        return (weights.at[0, pl.ds(0, parts - 1), :, span], w_held.at[pl.ds(0, parts - 1), :, span])

    inputs = [(pool, pool_twice.at[pl.ds(0, pool_count)]), half_of(0), (cotangent, scaled)]
    inputs += [half_of(h) for h in range(1, halves)]
    inputs += [(weights.at[0, parts - 1], w_held.at[parts - 1])]
    inputs += [(pool, pool_twice.at[pl.ds(pool_count, pool_count)])]
    arrivals = [
        pltpu.make_async_copy(src, dst, in_sem.at[i]) for i, (src, dst) in enumerate(inputs)
    ]
    for arrival in arrivals:
        arrival.start()
    pick_rows()
    clear()
    lax.fori_loop(0, plane, tabulate, 0)

    arrivals[0].wait()
    arrivals[1].wait()
    forward(0)
    arrivals[2].wait()
    long_tiles(scale_rows)
    make(0, 0, layers)
    meet()
    for j in range(group):
        scatter(j)
    loads()
    for h in range(1, halves):
        arrivals[2 + h].wait()
        forward(h)
        make(h, 0, layers)
        for j in range(group):
            scatter(h * group + j)
    is_end = (layer == 0) | (layer == last)

    def perform(i, op, lag, *extra):
        ch = i - lag
        valid = (ch >= 0) & (ch < chunks)
        if op == "ends":

            @pl.when(valid & is_end)
            def _():
                collect(ch)

                def one(q, carry):
                    pass_on(ch, q)
                    return carry

                lax.fori_loop(0, last, one, 0)

        if op == "mids":

            @pl.when(valid & jnp.logical_not(is_end))
            def _():
                if extra[0] == 0:
                    collect(ch)
                pass_on(ch, extra[0])

        if op == "update":

            @pl.when(valid)
            def _():
                update(ch)

        if op == "refill":

            @pl.when(valid)
            def _():
                refill(ch)

        if op == "relay":

            @pl.when(valid)
            def _():
                relay(ch, extra[0])

    def body(i, carry):
        ch = i + halves * group - START - group

        @pl.when((ch >= halves * group) & (ch < chunks))
        def _():
            scatter(ch)

        for step in ORDER:
            perform(i, *step)

        @pl.when(i == -1)
        def _():
            arrivals[-2].wait()
            long_tiles(backward)

        @pl.when(i == 0)
        def _():
            arrivals[-1].wait()
            for j in range(3):
                drain(states[j], load_sem.at[j])
            sum_tokens()

        unit = (i - START) // group + halves
        count = max(1, layers // group)

        @pl.when((i >= START) & (unit * group < chunks))
        def _():
            make(unit, (i - START) % group * count, count)

        token_grads(i - chunks * 3 // 4)
        return carry

    lags = [step[1] for step in ORDER]
    lax.fori_loop(min(lags), chunks + max(lags), body, 0)

    def finish(ch, carry):
        drain(inbox.at[ch, pl.ds(0, layers - 1)], part_send)
        drain(inbox.at[ch, 0], fresh_send)

        @pl.when(has_below & has_above)
        def _():
            drain(inbox.at[ch, pl.ds(0, layers)], fresh_send)

        return carry

    lax.fori_loop(0, chunks, finish, 0)
    drain(next_out.at[:, :, pl.ds(0, plane - 1)], out_send)
    drain(next_out.at[:, :, pl.ds(0, plane - 1)], out_recv)


def put(*refs):
    half = len(refs) // 2
    sems = refs[-1]
    copies = [
        pltpu.make_async_copy(refs[i], refs[half + i], sems.at[i]) for i in range(half)
    ]
    for copy in copies:
        copy.start()
    for copy in copies:
        copy.wait()


def settle(*arrays):
    return pl.pallas_call(
        put,
        out_shape=tuple(jax.ShapeDtypeStruct(a.shape, a.dtype) for a in arrays),
        in_specs=[pl.BlockSpec(memory_space=pltpu.VMEM)] * len(arrays),
        out_specs=(pl.BlockSpec(memory_space=pl.ANY),) * len(arrays),
        scratch_shapes=[pltpu.SemaphoreType.DMA((len(arrays),))],
        compiler_params=pltpu.CompilerParams(vmem_limit_bytes=1024 * 1024),
    )(*arrays)


def local(
    pool_tokens,
    cotangent,
    slot_weights,
    row_index,
    route_weight,
    slot_expert,
    next_expert,
    master,
    moment_m,
    moment_v,
):
    narrow_count = lax.axis_size("narrow")
    members = lax.axis_size("wide") * narrow_count
    parts, width, hidden_units = slot_weights.shape[1:]
    experts = master.shape[0]
    block = width // members
    length = row_index.shape[1]
    pool_count = pool_tokens.shape[0]
    plane = members // LAYERS
    cols = CHUNK_COLS
    split = min(SPLIT, max(1, block // ROW_TILE))
    piece = block // split
    chunks = parts * (hidden_units // cols) * split
    anywhere = pl.BlockSpec(memory_space=pl.ANY)
    scalars = pl.BlockSpec(memory_space=pltpu.SMEM)
    dma = pltpu.SemaphoreType.DMA
    bf16 = jnp.bfloat16
    state = pltpu.VMEM(master.shape, jnp.float32)
    held = pl.BlockSpec(memory_space=pltpu.VMEM)
    fresh, first, second, refilled, token_grads = pl.pallas_call(
        functools.partial(exchange, narrow_count, members),
        out_shape=(
            state,
            state,
            state,
            pltpu.VMEM((parts, LAYERS, plane, block, hidden_units), bf16),
            pltpu.VMEM(pool_tokens.shape, bf16),
        ),
        in_specs=[scalars, scalars, held, held] + [anywhere] * 6,
        out_specs=(held,) * 5,
        scratch_shapes=[
            pltpu.SMEM((experts * plane,), jnp.float32),
            pltpu.VMEM((chunks, plane, LAYERS, piece, cols), bf16),
            pltpu.VMEM((2 * pool_count, width), bf16),
            pltpu.VMEM((length, width), bf16),
            pltpu.VMEM((length, hidden_units), bf16),
            pltpu.VMEM((parts - 1, length, hidden_units), bf16),
            pltpu.VMEM((pool_count, length), bf16),
            pltpu.VMEM((length, 128), jnp.float32),
            pltpu.VMEM((2, length, hidden_units), jnp.float32),
            pltpu.VMEM((parts, width, hidden_units), bf16),
            pltpu.VMEM((2, 2 * pool_count, hidden_units), bf16),
            pltpu.VMEM((chunks, plane, LAYERS, piece, cols), bf16),
            pltpu.VMEM((chunks, LAYERS + 1, experts, piece, cols), bf16),
            pltpu.VMEM((LAYERS, experts, piece, cols), bf16),
            dma((4 + hidden_units // (UNIT * cols),)),
            dma((3,)),
            dma((chunks,)),
            dma((chunks,)),
            dma((chunks,)),
            dma,
            dma((chunks, LAYERS + 1)),
            dma,
            dma((chunks, LAYERS)),
            dma,
            dma,
        ],
        compiler_params=pltpu.CompilerParams(
            collective_id=0, has_side_effects=True, vmem_limit_bytes=46 * 1024 * 1024
        ),
    )(
        slot_expert[:, 0],
        next_expert[:, 0],
        row_index,
        route_weight,
        pool_tokens,
        cotangent,
        slot_weights,
        master,
        moment_m,
        moment_v,
    )
    next_weights = refilled.reshape(1, parts, width, hidden_units)
    return settle(token_grads, fresh, first, second, next_weights)


def solution(mesh):
    in_specs = (
        P(("wide", "narrow"), None),
        P(("wide", "narrow"), None),
        P(("wide", "narrow"), None, None, None),
        P(("wide", "narrow"), None),
        P(("wide", "narrow"), None),
        P(),
        P(),
        P(None, None, ("wide", "narrow"), None),
        P(None, None, ("wide", "narrow"), None),
        P(None, None, ("wide", "narrow"), None),
    )
    out_specs = (
        P(("wide", "narrow"), None),
        P(None, None, ("wide", "narrow"), None),
        P(None, None, ("wide", "narrow"), None),
        P(None, None, ("wide", "narrow"), None),
        P(("wide", "narrow"), None, None, None),
    )
    return jax.shard_map(local, mesh=mesh, in_specs=in_specs, out_specs=out_specs, check_vma=False)
```

```python
import functools

import jax
import jax.numpy as jnp
from jax import lax
from jax.experimental import pallas as pl
from jax.experimental.pallas import tpu as pltpu
from jax.sharding import PartitionSpec as P

MESH = pl.DeviceIdType.MESH
LAYERS = 4
CHUNK_COLS = 128
UNIT = 2
ROW_TILE = 16
WIDE_TILE = 512
LONG_TILE = 384
UNROLL = 8
SPLIT = 2
START = 1
DIRECT = 1
ORDER = (
    ("ends", -1),
    ("mids", 0, 0),
    ("relay", 4, 3),
    ("relay", 3, 2),
    ("relay", 2, 1),
    ("refill", 3, 0),
    ("update", 1),
    ("mids", 0, 2),
    ("mids", 0, 1),
    ("refill", 4, 1),
)


def inner(left, right):
    return lax.dot_general(
        left, right, (((0,), (0,)), ((), ())), preferred_element_type=jnp.float32
    )


def against(left, right):
    return lax.dot_general(
        left, right, (((1,), (1,)), ((), ())), preferred_element_type=jnp.float32
    )


def drain(ref, sem):
    pltpu.make_async_copy(ref, ref, sem).wait()


def exchange(
    narrow_count,
    members,
    experts_now,
    nexts,
    row_index,
    route,
    pool,
    cotangent,
    weights,
    master,
    moment_m,
    moment_v,
    master_out,
    m_out,
    v_out,
    next_out,
    tokens_out,
    owners,
    made,
    pool_twice,
    scaled,
    hidden,
    d_held,
    spread,
    route_column,
    gates,
    w_held,
    token_sums,
    recv,
    inbox,
    shelf,
    in_sem,
    load_sem,
    own_sem,
    a2a_send,
    a2a_recv,
    part_send,
    part_recv,
    fresh_send,
    fresh_recv,
    out_send,
    out_recv,
):
    experts, parts, block, hidden_units = master_out.shape
    chunks, plane, layers, piece_rows, cols = made.shape
    split = block // piece_rows
    group = UNIT * split
    per_part = hidden_units // cols * split
    width = w_held.shape[1]
    length = scaled.shape[0]
    pool_count = tokens_out.shape[0]
    scale_in = width ** (-0.5)
    scale_out = hidden_units ** (-0.5)
    states = (master_out, m_out, v_out)
    last = layers - 1
    me = lax.axis_index("wide") * narrow_count + lax.axis_index("narrow")
    layer = me // plane
    spot = me % plane
    base = layer * plane
    has_below = layer > 0
    has_above = layer < last
    is_end = (layer == 0) | (layer == last)

    def device(index):
        return (index // narrow_count, index % narrow_count)

    def peer_of(step):
        peer = spot + step
        return jnp.where(peer >= plane, peer - plane, peer)

    def others(body):
        if plane <= UNROLL:
            for step in range(1, plane):
                body(peer_of(step))
        else:

            def one(step, carry):
                body(peer_of(step))
                return carry

            lax.fori_loop(1, plane, one, 0)

    def part_of(ch):
        return (ch // per_part + parts - 1) % parts

    def cols_of(ch):
        return pl.ds(pl.multiple_of((ch % per_part) // split * cols, cols), cols)

    def rows_of(ch, start=0, size=piece_rows):
        first = (ch % split) * piece_rows + start
        return pl.ds(pl.multiple_of(first, size), size)

    barrier = pltpu.get_barrier_semaphore()

    def hello(index):
        pl.semaphore_signal(barrier, inc=1, device_id=device(index), device_id_type=MESH)

    others(lambda peer: hello(base + peer))

    def column(body):
        for step in range(1, layers):
            there = layer + step
            body(jnp.where(there > last, there - layers, there))

    column(lambda there: hello(there * plane + spot))

    def meet():
        pl.semaphore_wait(barrier, plane - 1 + layers - 1)

    def tiles_of(size, most, body):
        tile = min(most, size)

        def step(t, carry):
            body(pl.ds(pl.multiple_of(t * tile, tile), tile))
            return carry

        lax.fori_loop(0, size // tile, step, 0)

    def wide_tiles(body):
        tiles_of(width, WIDE_TILE, body)

    def long_tiles(body):
        tiles_of(length, LONG_TILE, body)

    def product_of(left, right):
        return jnp.dot(left, right, preferred_element_type=jnp.float32)

    def pick_rows():
        tokens = lax.broadcasted_iota(jnp.int32, spread.shape, 0)
        spread[...] = jnp.where(tokens == row_index[...], 1.0, 0.0).astype(jnp.bfloat16)
        route_column[...] = jnp.transpose(jnp.broadcast_to(route[...], (128, length)))

    def forward(h):
        span = pl.ds(pl.multiple_of(h * (UNIT * cols), UNIT * cols), UNIT * cols)
        for j in range(parts - 1):
            value = product_of(pool_twice[pl.ds(0, pool_count), :], w_held[j, :, span]) * scale_in
            high = value.astype(jnp.bfloat16)
            low = (value - high.astype(jnp.float32)).astype(jnp.bfloat16)
            gates[j, :, span] = inner(spread[...], high) + inner(spread[...], low)

        def finish_rows(rows):
            gate = gates[0, rows, span]
            upper = gates[1, rows, span]
            hidden[rows, span] = (gate * jax.nn.sigmoid(gate) * upper).astype(jnp.bfloat16)

        long_tiles(finish_rows)

    def scale_rows(span):
        column = route_column[span, pl.ds(0, 1)]
        scaled[span, :] = (column * scaled[span, :].astype(jnp.float32)).astype(jnp.bfloat16)

    def backward(span):
        back = product_of(scaled[span, :], w_held[2]) * scale_out
        gate = gates[0, span, :]
        upper = gates[1, span, :]
        sigma = jax.nn.sigmoid(gate)
        slope = sigma * (1.0 + gate * (1.0 - sigma))
        d_held[0, span, :] = (back * upper * slope).astype(jnp.bfloat16)
        d_held[1, span, :] = (back * (gate * sigma)).astype(jnp.bfloat16)

    def sum_tokens():
        for k in range(parts - 1):
            value = product_of(spread[...], d_held[k])
            high = value.astype(jnp.bfloat16)
            token_sums[k, pl.ds(0, pool_count), :] = high
            low = value - high.astype(jnp.float32)
            token_sums[k, pl.ds(pool_count, pool_count), :] = low.astype(jnp.bfloat16)

    def make(unit, first, count):
        ch = unit * group
        k = part_of(ch)
        start = pl.multiple_of((ch % per_part) // split * cols, UNIT * cols)
        right_span = pl.ds(start, UNIT * cols)

        def of_layer(l, left, right, scale):
            product = (inner(left, right) * scale).astype(jnp.bfloat16)
            for j in range(UNIT):
                piece = product[:, j * cols : (j + 1) * cols]
                piece = piece.reshape(plane, split, piece_rows, cols)
                for r in range(split):
                    made[ch + j * split + r, :, l] = piece[:, r]

        def span_of(l):
            return pl.ds(pl.multiple_of(l * (plane * block), plane * block), plane * block)

        @pl.when(k == parts - 1)
        def _():
            def down(l, carry):
                of_layer(l, scaled[:, span_of(l)], hidden[:, right_span], scale_out)
                return carry

            lax.fori_loop(first, first + count, down, 0)

        @pl.when(k != parts - 1)
        def _():
            def into(l, carry):
                of_layer(l, pool_twice[:, span_of(l)], token_sums[k, :, right_span], scale_in)
                return carry

            lax.fori_loop(first, first + count, into, 0)

    def scatter(ch):
        def send(peer):
            pltpu.make_async_remote_copy(
                src_ref=made.at[ch, peer],
                dst_ref=recv.at[ch, spot],
                send_sem=a2a_send.at[ch],
                recv_sem=a2a_recv.at[ch],
                device_id=device(base + peer),
                device_id_type=MESH,
            ).start()

        others(send)
        pltpu.make_async_copy(made.at[ch, spot], recv.at[ch, spot], own_sem.at[ch]).start()

    def scatter_layer(ch, l):
        def send(peer):
            pltpu.make_async_remote_copy(
                src_ref=made.at[ch, peer, l],
                dst_ref=recv.at[ch, spot, l],
                send_sem=a2a_send.at[ch],
                recv_sem=a2a_recv.at[ch],
                device_id=device(base + peer),
                device_id_type=MESH,
            ).start()

        others(send)
        pltpu.make_async_copy(made.at[ch, spot, l], recv.at[ch, spot, l], own_sem.at[ch]).start()

    def collect(ch):
        drain(recv.at[ch, pl.ds(0, plane - 1)], a2a_recv.at[ch])
        drain(recv.at[ch, 0], own_sem.at[ch])

    def tabulate(s, carry):
        for e in range(experts):
            owners[e * plane + s] = jnp.where(experts_now[base + s] == e, 1.0, 0.0)
        return carry

    row_tile = min(ROW_TILE, piece_rows)

    def row_tiles(body):
        def step(t, carry):
            body(pl.multiple_of(t * row_tile, row_tile))
            return carry

        lax.fori_loop(0, piece_rows // row_tile, step, 0)

    def sums(ch, l, rows, init):
        def add(outer, totals):
            for u in range(UNROLL):
                s = outer * UNROLL + u
                value = recv[ch, s, l, rows, :].astype(jnp.float32)
                totals = tuple(
                    total + value * owners[e * plane + s] for e, total in enumerate(totals)
                )
            return totals

        return lax.fori_loop(0, plane // UNROLL, add, init)

    def pass_on(ch, q):
        low = layer * 2 < layers
        ups = last - layer
        up = jnp.where(low, q < ups, q >= layer)
        l = jnp.where(
            low,
            jnp.where(q < ups, last - q, q - ups),
            jnp.where(q < layer, q, last - (q - layer)),
        )
        fed = jnp.where(up, has_below, has_above)
        target = jnp.where(up, me + plane, me - plane)
        place = jnp.where(up, l, jnp.where(l == layer - 1, layers, l))

        @pl.when(fed)
        def _():
            drain(inbox.at[0, 0], part_recv.at[ch, l])

        def body(start):
            rows = pl.ds(start, row_tile)
            init = tuple(inbox[ch, l, e, rows, :].astype(jnp.float32) for e in range(experts))
            totals = sums(ch, l, rows, init)
            for e, total in enumerate(totals):
                recv[ch, e, l, rows, :] = total.astype(jnp.bfloat16)

        row_tiles(body)
        pltpu.make_async_remote_copy(
            src_ref=recv.at[ch, pl.ds(0, experts), l],
            dst_ref=inbox.at[ch, place],
            send_sem=part_send,
            recv_sem=part_recv.at[ch, place],
            device_id=device(target),
            device_id_type=MESH,
        ).start()

    def direct(ch):
        return ch >= chunks - DIRECT

    def hand(ch, l, target):
        pltpu.make_async_remote_copy(
            src_ref=inbox.at[ch, l],
            dst_ref=inbox.at[ch, l],
            send_sem=fresh_send,
            recv_sem=fresh_recv.at[ch, l],
            device_id=device(target),
            device_id_type=MESH,
        ).start()

    def fill(ch, first, count):
        k = part_of(ch)
        span = cols_of(ch)
        rows = rows_of(ch)
        for t in range(count):
            shelf[t] = inbox[ch, first + t]

        def give(peer):
            which = nexts[base + peer]
            for t in range(count):
                made[ch, peer, first + t] = shelf[t, which]
            pltpu.make_async_remote_copy(
                src_ref=made.at[ch, peer, pl.ds(first, count)],
                dst_ref=next_out.at[k, pl.ds(first, count), spot, rows, span],
                send_sem=out_send,
                recv_sem=out_recv,
                device_id=device(base + peer),
                device_id_type=MESH,
            ).start()

        others(give)
        which = nexts[me]
        for t in range(count):
            next_out[k, first + t, spot, rows, span] = shelf[t, which]

    def refill(ch, far):
        if far:

            @pl.when(is_end)
            def _():
                fill(ch, last - layer, 1)

        else:
            drain(recv.at[ch, pl.ds(0, plane - 1)], a2a_send.at[ch])

            @pl.when(is_end)
            def _():
                fill(ch, jnp.where(layer == 0, 0, 1), last)

            @pl.when(jnp.logical_not(is_end))
            def _():
                fill(ch, 0, layers)

    def update(ch):
        k = part_of(ch)
        span = cols_of(ch)

        @pl.when(has_below)
        def _():
            drain(inbox.at[0, 0], part_recv.at[ch, layer])

        @pl.when(has_above)
        def _():
            drain(inbox.at[0, 0], part_recv.at[ch, layers])

        def body(start):
            rows = pl.ds(start, row_tile)
            state_rows = rows_of(ch, start, row_tile)
            init = tuple(
                inbox[ch, layer, e, rows, :].astype(jnp.float32)
                + inbox[ch, layers, e, rows, :].astype(jnp.float32)
                for e in range(experts)
            )
            totals = sums(ch, layer, rows, init)
            for e, grad in enumerate(totals):
                held = states[0][e, k, state_rows, span]
                first = 0.9 * states[1][e, k, state_rows, span] + 0.1 * grad
                second = 0.95 * states[2][e, k, state_rows, span] + 0.05 * grad * grad
                value = held - 0.05 * (first / (jnp.sqrt(second) + 1e-08) + 0.1 * held)
                states[0][e, k, state_rows, span] = value
                states[1][e, k, state_rows, span] = first
                states[2][e, k, state_rows, span] = second
                inbox[ch, layer, e, rows, :] = value.astype(jnp.bfloat16)

        row_tiles(body)

        @pl.when(direct(ch))
        def _():
            column(lambda there: hand(ch, layer, there * plane + spot))

        @pl.when(jnp.logical_not(direct(ch)) & has_above)
        def _():
            hand(ch, layer, me + plane)

        @pl.when(jnp.logical_not(direct(ch)) & has_below)
        def _():
            hand(ch, layer, me - plane)


    def relay(ch, hop):
        below = layer - hop
        above = layer + hop

        @pl.when(below >= 0)
        def _():
            drain(inbox.at[0, 0], fresh_recv.at[ch, below])

            @pl.when(jnp.logical_not(direct(ch)) & has_above)
            def _():
                hand(ch, below, me + plane)

        @pl.when(above <= last)
        def _():
            drain(inbox.at[0, 0], fresh_recv.at[ch, above])

            @pl.when(jnp.logical_not(direct(ch)) & has_below)
            def _():
                hand(ch, above, me - plane)

    def loads():
        for i, ref in enumerate((master, moment_m, moment_v)):
            pltpu.make_async_copy(ref, states[i], load_sem.at[i]).start()

    def clear():
        zero = jnp.zeros((experts, piece_rows, cols), jnp.bfloat16)

        @pl.when(layer == 0)
        def _():
            def wipe(t, carry):
                inbox[t // layers, t % layers] = zero
                return carry

            lax.fori_loop(0, chunks * layers, wipe, 0)

        @pl.when(layer == last)
        def _():
            def wipe(t, carry):
                inbox[t // layers, jnp.where(t % layers == last, layers, t % layers)] = zero
                return carry

            lax.fori_loop(0, chunks * layers, wipe, 0)

    def token_grads(piece):
        tile = min(WIDE_TILE, width)

        @pl.when((piece >= 0) & (piece < width // tile))
        def _():
            span = pl.ds(pl.multiple_of(piece * tile, tile), tile)
            total = against(token_sums[0, pl.ds(0, pool_count), :], w_held[0, span, :])
            total = total + against(token_sums[1, pl.ds(0, pool_count), :], w_held[1, span, :])
            tokens_out[:, span] = (total * scale_in).astype(jnp.bfloat16)

    halves = hidden_units // (UNIT * cols)

    def half_of(h):
        span = pl.ds(h * (UNIT * cols), UNIT * cols)
        return (weights.at[0, pl.ds(0, parts - 1), :, span], w_held.at[pl.ds(0, parts - 1), :, span])

    inputs = [(pool, pool_twice.at[pl.ds(0, pool_count)]), half_of(0), (cotangent, scaled)]
    inputs += [half_of(h) for h in range(1, halves)]
    inputs += [(weights.at[0, parts - 1], w_held.at[parts - 1])]
    inputs += [(pool, pool_twice.at[pl.ds(pool_count, pool_count)])]
    arrivals = [
        pltpu.make_async_copy(src, dst, in_sem.at[i]) for i, (src, dst) in enumerate(inputs)
    ]
    for arrival in arrivals[:3]:
        arrival.start()
    pick_rows()
    clear()
    lax.fori_loop(0, plane, tabulate, 0)

    arrivals[0].wait()
    arrivals[1].wait()
    for arrival in arrivals[3:]:
        arrival.start()
    forward(0)
    arrivals[2].wait()
    long_tiles(scale_rows)
    make(0, 0, 1)
    meet()
    scatter_layer(0, 0)
    for l in range(1, layers):
        make(0, l, 1)
        scatter_layer(0, l)
    for j in range(1, group):
        scatter(j)
    loads()
    for h in range(1, halves):
        arrivals[2 + h].wait()
        forward(h)
        make(h, 0, layers)
        for j in range(group):
            scatter(h * group + j)

    def perform(i, op, lag, *extra):
        ch = i - lag
        valid = (ch >= 0) & (ch < chunks)
        if op == "ends":

            @pl.when(valid & is_end)
            def _():
                collect(ch)

                def one(q, carry):
                    pass_on(ch, q)
                    return carry

                lax.fori_loop(0, last, one, 0)

        if op == "mids":

            @pl.when(valid & jnp.logical_not(is_end))
            def _():
                if extra[0] == 0:
                    collect(ch)
                pass_on(ch, extra[0])

        if op == "update":

            @pl.when(valid)
            def _():
                update(ch)

        if op == "refill":

            @pl.when(valid)
            def _():
                refill(ch, extra[0])

        if op == "relay":

            @pl.when(valid)
            def _():
                relay(ch, extra[0])

    def body(i, carry):
        ch = i + halves * group - START - group

        @pl.when((ch >= halves * group) & (ch < chunks))
        def _():
            scatter(ch)

        for step in ORDER:
            perform(i, *step)

        @pl.when(i == -1)
        def _():
            arrivals[-2].wait()
            long_tiles(backward)

        @pl.when(i == 0)
        def _():
            arrivals[-1].wait()
            for j in range(3):
                drain(states[j], load_sem.at[j])
            sum_tokens()

        unit = (i - START) // group + halves
        count = max(1, layers // group)

        @pl.when((i >= START) & (unit * group < chunks))
        def _():
            make(unit, (i - START) % group * count, count)

        token_grads(i - chunks // 2)
        return carry

    lags = [step[1] for step in ORDER]
    lax.fori_loop(min(lags), chunks + max(lags), body, 0)

    def finish(ch, carry):
        drain(inbox.at[ch, pl.ds(0, layers - 1)], part_send)
        relayed = jnp.logical_not(direct(ch))

        @pl.when(direct(ch))
        def _():
            drain(inbox.at[ch, pl.ds(0, layers - 1)], fresh_send)

        @pl.when(relayed & is_end)
        def _():
            drain(inbox.at[ch, 0], fresh_send)

        @pl.when(relayed & jnp.logical_not(is_end))
        def _():
            drain(inbox.at[ch, pl.ds(0, layers + 1)], fresh_send)

        return carry

    lax.fori_loop(0, chunks, finish, 0)
    drain(next_out.at[:, :, pl.ds(0, plane - 1)], out_send)
    drain(next_out.at[:, :, pl.ds(0, plane - 1)], out_recv)


def put(*refs):
    half = len(refs) // 2
    sems = refs[-1]
    copies = [
        pltpu.make_async_copy(refs[i], refs[half + i], sems.at[i]) for i in range(half)
    ]
    for copy in copies:
        copy.start()
    for copy in copies:
        copy.wait()


def settle(*arrays):
    return pl.pallas_call(
        put,
        out_shape=tuple(jax.ShapeDtypeStruct(a.shape, a.dtype) for a in arrays),
        in_specs=[pl.BlockSpec(memory_space=pltpu.VMEM)] * len(arrays),
        out_specs=(pl.BlockSpec(memory_space=pl.ANY),) * len(arrays),
        scratch_shapes=[pltpu.SemaphoreType.DMA((len(arrays),))],
        compiler_params=pltpu.CompilerParams(vmem_limit_bytes=1024 * 1024),
    )(*arrays)


def local(
    pool_tokens,
    cotangent,
    slot_weights,
    row_index,
    route_weight,
    slot_expert,
    next_expert,
    master,
    moment_m,
    moment_v,
):
    narrow_count = lax.axis_size("narrow")
    members = lax.axis_size("wide") * narrow_count
    parts, width, hidden_units = slot_weights.shape[1:]
    experts = master.shape[0]
    block = width // members
    length = row_index.shape[1]
    pool_count = pool_tokens.shape[0]
    plane = members // LAYERS
    cols = CHUNK_COLS
    split = min(SPLIT, max(1, block // ROW_TILE))
    piece = block // split
    chunks = parts * (hidden_units // cols) * split
    anywhere = pl.BlockSpec(memory_space=pl.ANY)
    scalars = pl.BlockSpec(memory_space=pltpu.SMEM)
    dma = pltpu.SemaphoreType.DMA
    bf16 = jnp.bfloat16
    state = pltpu.VMEM(master.shape, jnp.float32)
    held = pl.BlockSpec(memory_space=pltpu.VMEM)
    fresh, first, second, refilled, token_grads = pl.pallas_call(
        functools.partial(exchange, narrow_count, members),
        out_shape=(
            state,
            state,
            state,
            pltpu.VMEM((parts, LAYERS, plane, block, hidden_units), bf16),
            pltpu.VMEM(pool_tokens.shape, bf16),
        ),
        in_specs=[scalars, scalars, held, held] + [anywhere] * 6,
        out_specs=(held,) * 5,
        scratch_shapes=[
            pltpu.SMEM((experts * plane,), jnp.float32),
            pltpu.VMEM((chunks, plane, LAYERS, piece, cols), bf16),
            pltpu.VMEM((2 * pool_count, width), bf16),
            pltpu.VMEM((length, width), bf16),
            pltpu.VMEM((length, hidden_units), bf16),
            pltpu.VMEM((parts - 1, length, hidden_units), bf16),
            pltpu.VMEM((pool_count, length), bf16),
            pltpu.VMEM((length, 128), jnp.float32),
            pltpu.VMEM((2, length, hidden_units), jnp.float32),
            pltpu.VMEM((parts, width, hidden_units), bf16),
            pltpu.VMEM((2, 2 * pool_count, hidden_units), bf16),
            pltpu.VMEM((chunks, plane, LAYERS, piece, cols), bf16),
            pltpu.VMEM((chunks, LAYERS + 1, experts, piece, cols), bf16),
            pltpu.VMEM((LAYERS, experts, piece, cols), bf16),
            dma((4 + hidden_units // (UNIT * cols),)),
            dma((3,)),
            dma((chunks,)),
            dma((chunks,)),
            dma((chunks,)),
            dma,
            dma((chunks, LAYERS + 1)),
            dma,
            dma((chunks, LAYERS)),
            dma,
            dma,
        ],
        compiler_params=pltpu.CompilerParams(
            collective_id=0, has_side_effects=True, vmem_limit_bytes=46 * 1024 * 1024
        ),
    )(
        slot_expert[:, 0],
        next_expert[:, 0],
        row_index,
        route_weight,
        pool_tokens,
        cotangent,
        slot_weights,
        master,
        moment_m,
        moment_v,
    )
    next_weights = refilled.reshape(1, parts, width, hidden_units)
    return settle(token_grads, fresh, first, second, next_weights)


def solution(mesh):
    in_specs = (
        P(("wide", "narrow"), None),
        P(("wide", "narrow"), None),
        P(("wide", "narrow"), None, None, None),
        P(("wide", "narrow"), None),
        P(("wide", "narrow"), None),
        P(),
        P(),
        P(None, None, ("wide", "narrow"), None),
        P(None, None, ("wide", "narrow"), None),
        P(None, None, ("wide", "narrow"), None),
    )
    out_specs = (
        P(("wide", "narrow"), None),
        P(None, None, ("wide", "narrow"), None),
        P(None, None, ("wide", "narrow"), None),
        P(None, None, ("wide", "narrow"), None),
        P(("wide", "narrow"), None, None, None),
    )
    return jax.shard_map(local, mesh=mesh, in_specs=in_specs, out_specs=out_specs, check_vma=False)
```

```python
import functools

import jax
import jax.numpy as jnp
from jax import lax
from jax.experimental import pallas as pl
from jax.experimental.pallas import tpu as pltpu
from jax.sharding import PartitionSpec as P

MESH = pl.DeviceIdType.MESH
LAYERS = 4
CHUNK_COLS = 128
UNIT = 2
ROW_TILE = 16
WIDE_TILE = 512
LONG_TILE = 384
UNROLL = 8
SPLIT = 2
START = 1
DIRECT = 1
ORDER = (
    ("ends", -1, 0, 2),
    ("mids", 0, 0),
    ("relay", 4, 3),
    ("relay", 3, 2),
    ("relay", 2, 1),
    ("refill", 3, 0),
    ("update", 1),
    ("ends", -1, 2, 9),
    ("mids", 0, 2),
    ("mids", 0, 1),
    ("refill", 4, 1),
)


def inner(left, right):
    return lax.dot_general(
        left, right, (((0,), (0,)), ((), ())), preferred_element_type=jnp.float32
    )


def against(left, right):
    return lax.dot_general(
        left, right, (((1,), (1,)), ((), ())), preferred_element_type=jnp.float32
    )


def drain(ref, sem):
    pltpu.make_async_copy(ref, ref, sem).wait()


def exchange(
    narrow_count,
    members,
    experts_now,
    nexts,
    row_index,
    route,
    pool,
    cotangent,
    weights,
    master,
    moment_m,
    moment_v,
    master_out,
    m_out,
    v_out,
    next_out,
    tokens_out,
    owners,
    made,
    pool_twice,
    scaled,
    hidden,
    d_held,
    spread,
    route_column,
    gates,
    w_held,
    token_sums,
    recv,
    inbox,
    shelf,
    in_sem,
    load_sem,
    own_sem,
    a2a_send,
    a2a_recv,
    part_send,
    part_recv,
    fresh_send,
    fresh_recv,
    out_send,
    out_recv,
):
    experts, parts, block, hidden_units = master_out.shape
    chunks, plane, layers, piece_rows, cols = made.shape
    split = block // piece_rows
    group = UNIT * split
    per_part = hidden_units // cols * split
    width = w_held.shape[1]
    length = scaled.shape[0]
    pool_count = tokens_out.shape[0]
    scale_in = width ** (-0.5)
    scale_out = hidden_units ** (-0.5)
    states = (master_out, m_out, v_out)
    last = layers - 1
    me = lax.axis_index("wide") * narrow_count + lax.axis_index("narrow")
    layer = me // plane
    spot = me % plane
    base = layer * plane
    has_below = layer > 0
    has_above = layer < last
    is_end = (layer == 0) | (layer == last)

    def device(index):
        return (index // narrow_count, index % narrow_count)

    def peer_of(step):
        peer = spot + step
        return jnp.where(peer >= plane, peer - plane, peer)

    def others(body):
        if plane <= UNROLL:
            for step in range(1, plane):
                body(peer_of(step))
        else:

            def one(step, carry):
                body(peer_of(step))
                return carry

            lax.fori_loop(1, plane, one, 0)

    def part_of(ch):
        return (ch // per_part + parts - 1) % parts

    def cols_of(ch):
        return pl.ds(pl.multiple_of((ch % per_part) // split * cols, cols), cols)

    def rows_of(ch, start=0, size=piece_rows):
        first = (ch % split) * piece_rows + start
        return pl.ds(pl.multiple_of(first, size), size)

    barrier = pltpu.get_barrier_semaphore()

    def hello(index):
        pl.semaphore_signal(barrier, inc=1, device_id=device(index), device_id_type=MESH)

    others(lambda peer: hello(base + peer))

    def column(body):
        for step in range(1, layers):
            there = layer + step
            body(jnp.where(there > last, there - layers, there))

    column(lambda there: hello(there * plane + spot))

    def meet():
        pl.semaphore_wait(barrier, plane - 1 + layers - 1)

    def tiles_of(size, most, body):
        tile = min(most, size)

        def step(t, carry):
            body(pl.ds(pl.multiple_of(t * tile, tile), tile))
            return carry

        lax.fori_loop(0, size // tile, step, 0)

    def wide_tiles(body):
        tiles_of(width, WIDE_TILE, body)

    def long_tiles(body):
        tiles_of(length, LONG_TILE, body)

    def product_of(left, right):
        return jnp.dot(left, right, preferred_element_type=jnp.float32)

    def pick_rows():
        tokens = lax.broadcasted_iota(jnp.int32, spread.shape, 0)
        spread[...] = jnp.where(tokens == row_index[...], 1.0, 0.0).astype(jnp.bfloat16)
        route_column[...] = jnp.transpose(jnp.broadcast_to(route[...], (128, length)))

    def forward(h):
        span = pl.ds(pl.multiple_of(h * (UNIT * cols), UNIT * cols), UNIT * cols)
        for j in range(parts - 1):
            value = product_of(pool_twice[pl.ds(0, pool_count), :], w_held[j, :, span]) * scale_in
            high = value.astype(jnp.bfloat16)
            low = (value - high.astype(jnp.float32)).astype(jnp.bfloat16)
            gates[j, :, span] = inner(spread[...], high) + inner(spread[...], low)

        def finish_rows(rows):
            gate = gates[0, rows, span]
            upper = gates[1, rows, span]
            hidden[rows, span] = (gate * jax.nn.sigmoid(gate) * upper).astype(jnp.bfloat16)

        long_tiles(finish_rows)

    def scale_rows(span):
        column = route_column[span, pl.ds(0, 1)]
        scaled[span, :] = (column * scaled[span, :].astype(jnp.float32)).astype(jnp.bfloat16)

    def backward(span):
        back = product_of(scaled[span, :], w_held[2]) * scale_out
        gate = gates[0, span, :]
        upper = gates[1, span, :]
        sigma = jax.nn.sigmoid(gate)
        slope = sigma * (1.0 + gate * (1.0 - sigma))
        d_held[0, span, :] = (back * upper * slope).astype(jnp.bfloat16)
        d_held[1, span, :] = (back * (gate * sigma)).astype(jnp.bfloat16)

    def sum_tokens():
        for k in range(parts - 1):
            value = product_of(spread[...], d_held[k])
            high = value.astype(jnp.bfloat16)
            token_sums[k, pl.ds(0, pool_count), :] = high
            low = value - high.astype(jnp.float32)
            token_sums[k, pl.ds(pool_count, pool_count), :] = low.astype(jnp.bfloat16)

    def make(unit, first, count):
        ch = unit * group
        k = part_of(ch)
        start = pl.multiple_of((ch % per_part) // split * cols, UNIT * cols)
        right_span = pl.ds(start, UNIT * cols)

        def of_layer(l, left, right, scale):
            product = (inner(left, right) * scale).astype(jnp.bfloat16)
            for j in range(UNIT):
                piece = product[:, j * cols : (j + 1) * cols]
                piece = piece.reshape(plane, split, piece_rows, cols)
                for r in range(split):
                    made[ch + j * split + r, :, l] = piece[:, r]

        def span_of(l):
            return pl.ds(pl.multiple_of(l * (plane * block), plane * block), plane * block)

        @pl.when(k == parts - 1)
        def _():
            def down(l, carry):
                of_layer(l, scaled[:, span_of(l)], hidden[:, right_span], scale_out)
                return carry

            lax.fori_loop(first, first + count, down, 0)

        @pl.when(k != parts - 1)
        def _():
            def into(l, carry):
                of_layer(l, pool_twice[:, span_of(l)], token_sums[k, :, right_span], scale_in)
                return carry

            lax.fori_loop(first, first + count, into, 0)

    def scatter(ch):
        def send(peer):
            pltpu.make_async_remote_copy(
                src_ref=made.at[ch, peer],
                dst_ref=recv.at[ch, spot],
                send_sem=a2a_send.at[ch],
                recv_sem=a2a_recv.at[ch],
                device_id=device(base + peer),
                device_id_type=MESH,
            ).start()

        others(send)
        pltpu.make_async_copy(made.at[ch, spot], recv.at[ch, spot], own_sem.at[ch]).start()

    def scatter_layer(ch, l):
        def send(peer):
            pltpu.make_async_remote_copy(
                src_ref=made.at[ch, peer, l],
                dst_ref=recv.at[ch, spot, l],
                send_sem=a2a_send.at[ch],
                recv_sem=a2a_recv.at[ch],
                device_id=device(base + peer),
                device_id_type=MESH,
            ).start()

        others(send)
        pltpu.make_async_copy(made.at[ch, spot, l], recv.at[ch, spot, l], own_sem.at[ch]).start()

    def collect(ch):
        drain(recv.at[ch, pl.ds(0, plane - 1)], a2a_recv.at[ch])
        drain(recv.at[ch, 0], own_sem.at[ch])

    def tabulate(s, carry):
        for e in range(experts):
            owners[e * plane + s] = jnp.where(experts_now[base + s] == e, 1.0, 0.0)
        return carry

    row_tile = min(ROW_TILE, piece_rows)

    def row_tiles(body):
        def step(t, carry):
            body(pl.multiple_of(t * row_tile, row_tile))
            return carry

        lax.fori_loop(0, piece_rows // row_tile, step, 0)

    def sums(ch, l, rows, init):
        def add(outer, totals):
            for u in range(UNROLL):
                s = outer * UNROLL + u
                value = recv[ch, s, l, rows, :].astype(jnp.float32)
                totals = tuple(
                    total + value * owners[e * plane + s] for e, total in enumerate(totals)
                )
            return totals

        return lax.fori_loop(0, plane // UNROLL, add, init)

    def pass_on(ch, q):
        low = layer * 2 < layers
        ups = last - layer
        up = jnp.where(low, q < ups, q >= layer)
        l = jnp.where(
            low,
            jnp.where(q < ups, last - q, q - ups),
            jnp.where(q < layer, q, last - (q - layer)),
        )
        fed = jnp.where(up, has_below, has_above)
        target = jnp.where(up, me + plane, me - plane)
        place = jnp.where(up, l, jnp.where(l == layer - 1, layers, l))

        @pl.when(fed)
        def _():
            drain(inbox.at[0, 0], part_recv.at[ch, l])

        def body(start):
            rows = pl.ds(start, row_tile)
            init = tuple(inbox[ch, l, e, rows, :].astype(jnp.float32) for e in range(experts))
            totals = sums(ch, l, rows, init)
            for e, total in enumerate(totals):
                recv[ch, e, l, rows, :] = total.astype(jnp.bfloat16)

        row_tiles(body)
        pltpu.make_async_remote_copy(
            src_ref=recv.at[ch, pl.ds(0, experts), l],
            dst_ref=inbox.at[ch, place],
            send_sem=part_send,
            recv_sem=part_recv.at[ch, place],
            device_id=device(target),
            device_id_type=MESH,
        ).start()

    def direct(ch):
        return ch >= chunks - DIRECT

    def hand(ch, l, target):
        pltpu.make_async_remote_copy(
            src_ref=inbox.at[ch, l],
            dst_ref=inbox.at[ch, l],
            send_sem=fresh_send,
            recv_sem=fresh_recv.at[ch, l],
            device_id=device(target),
            device_id_type=MESH,
        ).start()

    def fill(ch, first, count):
        k = part_of(ch)
        span = cols_of(ch)
        rows = rows_of(ch)
        for t in range(count):
            shelf[t] = inbox[ch, first + t]

        def give(peer):
            which = nexts[base + peer]
            for t in range(count):
                made[ch, peer, first + t] = shelf[t, which]
            pltpu.make_async_remote_copy(
                src_ref=made.at[ch, peer, pl.ds(first, count)],
                dst_ref=next_out.at[k, pl.ds(first, count), spot, rows, span],
                send_sem=out_send,
                recv_sem=out_recv,
                device_id=device(base + peer),
                device_id_type=MESH,
            ).start()

        others(give)
        which = nexts[me]
        for t in range(count):
            next_out[k, first + t, spot, rows, span] = shelf[t, which]

    def refill(ch, far):
        if far:

            @pl.when(is_end)
            def _():
                fill(ch, last - layer, 1)

        else:
            drain(recv.at[ch, pl.ds(0, plane - 1)], a2a_send.at[ch])

            @pl.when(is_end)
            def _():
                fill(ch, jnp.where(layer == 0, 0, 1), last)

            @pl.when(jnp.logical_not(is_end))
            def _():
                fill(ch, 0, layers)

    def update(ch):
        k = part_of(ch)
        span = cols_of(ch)

        @pl.when(has_below)
        def _():
            drain(inbox.at[0, 0], part_recv.at[ch, layer])

        @pl.when(has_above)
        def _():
            drain(inbox.at[0, 0], part_recv.at[ch, layers])

        def body(start):
            rows = pl.ds(start, row_tile)
            state_rows = rows_of(ch, start, row_tile)
            init = tuple(
                inbox[ch, layer, e, rows, :].astype(jnp.float32)
                + inbox[ch, layers, e, rows, :].astype(jnp.float32)
                for e in range(experts)
            )
            totals = sums(ch, layer, rows, init)
            for e, grad in enumerate(totals):
                held = states[0][e, k, state_rows, span]
                first = 0.9 * states[1][e, k, state_rows, span] + 0.1 * grad
                second = 0.95 * states[2][e, k, state_rows, span] + 0.05 * grad * grad
                value = held - 0.05 * (first / (jnp.sqrt(second) + 1e-08) + 0.1 * held)
                states[0][e, k, state_rows, span] = value
                states[1][e, k, state_rows, span] = first
                states[2][e, k, state_rows, span] = second
                inbox[ch, layer, e, rows, :] = value.astype(jnp.bfloat16)

        row_tiles(body)

        @pl.when(direct(ch))
        def _():
            column(lambda there: hand(ch, layer, there * plane + spot))

        @pl.when(jnp.logical_not(direct(ch)) & has_above)
        def _():
            hand(ch, layer, me + plane)

        @pl.when(jnp.logical_not(direct(ch)) & has_below)
        def _():
            hand(ch, layer, me - plane)


    def relay(ch, hop):
        below = layer - hop
        above = layer + hop

        @pl.when(below >= 0)
        def _():
            drain(inbox.at[0, 0], fresh_recv.at[ch, below])

            @pl.when(jnp.logical_not(direct(ch)) & has_above)
            def _():
                hand(ch, below, me + plane)

        @pl.when(above <= last)
        def _():
            drain(inbox.at[0, 0], fresh_recv.at[ch, above])

            @pl.when(jnp.logical_not(direct(ch)) & has_below)
            def _():
                hand(ch, above, me - plane)

    def loads():
        for i, ref in enumerate((master, moment_m, moment_v)):
            pltpu.make_async_copy(ref, states[i], load_sem.at[i]).start()

    def clear():
        zero = jnp.zeros((experts, piece_rows, cols), jnp.bfloat16)

        @pl.when(layer == 0)
        def _():
            def wipe(t, carry):
                inbox[t // layers, t % layers] = zero
                return carry

            lax.fori_loop(0, chunks * layers, wipe, 0)

        @pl.when(layer == last)
        def _():
            def wipe(t, carry):
                inbox[t // layers, jnp.where(t % layers == last, layers, t % layers)] = zero
                return carry

            lax.fori_loop(0, chunks * layers, wipe, 0)

    def token_grads(piece):
        tile = min(WIDE_TILE, width)

        @pl.when((piece >= 0) & (piece < width // tile))
        def _():
            span = pl.ds(pl.multiple_of(piece * tile, tile), tile)
            total = against(token_sums[0, pl.ds(0, pool_count), :], w_held[0, span, :])
            total = total + against(token_sums[1, pl.ds(0, pool_count), :], w_held[1, span, :])
            tokens_out[:, span] = (total * scale_in).astype(jnp.bfloat16)

    halves = hidden_units // (UNIT * cols)

    def half_of(h):
        span = pl.ds(h * (UNIT * cols), UNIT * cols)
        return (weights.at[0, pl.ds(0, parts - 1), :, span], w_held.at[pl.ds(0, parts - 1), :, span])

    inputs = [(pool, pool_twice.at[pl.ds(0, pool_count)]), half_of(0), (cotangent, scaled)]
    inputs += [half_of(h) for h in range(1, halves)]
    inputs += [(weights.at[0, parts - 1], w_held.at[parts - 1])]
    inputs += [(pool, pool_twice.at[pl.ds(pool_count, pool_count)])]
    arrivals = [
        pltpu.make_async_copy(src, dst, in_sem.at[i]) for i, (src, dst) in enumerate(inputs)
    ]
    for arrival in arrivals[:3]:
        arrival.start()
    pick_rows()
    clear()
    lax.fori_loop(0, plane, tabulate, 0)

    arrivals[0].wait()
    arrivals[1].wait()
    for arrival in arrivals[3:]:
        arrival.start()
    forward(0)
    arrivals[2].wait()
    long_tiles(scale_rows)
    make(0, 0, 1)
    meet()
    scatter_layer(0, 0)
    for l in range(1, layers):
        make(0, l, 1)
        scatter_layer(0, l)
    for j in range(1, group):
        scatter(j)
    loads()
    for h in range(1, halves):
        arrivals[2 + h].wait()
        forward(h)
        make(h, 0, layers)
        for j in range(group):
            scatter(h * group + j)

    def perform(i, op, lag, *extra):
        ch = i - lag
        valid = (ch >= 0) & (ch < chunks)
        if op == "ends":

            @pl.when(valid & is_end)
            def _():
                if extra[0] == 0:
                    collect(ch)
                for q in range(extra[0], min(extra[1], last)):
                    pass_on(ch, q)

        if op == "mids":

            @pl.when(valid & jnp.logical_not(is_end))
            def _():
                if extra[0] == 0:
                    collect(ch)
                pass_on(ch, extra[0])

        if op == "update":

            @pl.when(valid)
            def _():
                update(ch)

        if op == "refill":

            @pl.when(valid)
            def _():
                refill(ch, extra[0])

        if op == "relay":

            @pl.when(valid)
            def _():
                relay(ch, extra[0])

    def body(i, carry):
        ch = i + halves * group - START - group

        @pl.when((ch >= halves * group) & (ch < chunks))
        def _():
            scatter(ch)

        for step in ORDER:
            perform(i, *step)

        @pl.when(i == -1)
        def _():
            arrivals[-2].wait()
            long_tiles(backward)

        @pl.when(i == 0)
        def _():
            arrivals[-1].wait()
            for j in range(3):
                drain(states[j], load_sem.at[j])
            sum_tokens()

        unit = (i - START) // group + halves
        count = max(1, layers // group)

        @pl.when((i >= START) & (unit * group < chunks))
        def _():
            make(unit, (i - START) % group * count, count)

        token_grads(i - chunks // 2)
        return carry

    lags = [step[1] for step in ORDER]
    lax.fori_loop(min(lags), chunks + max(lags), body, 0)

    def finish(ch, carry):
        drain(inbox.at[ch, pl.ds(0, layers - 1)], part_send)
        relayed = jnp.logical_not(direct(ch))

        @pl.when(direct(ch))
        def _():
            drain(inbox.at[ch, pl.ds(0, layers - 1)], fresh_send)

        @pl.when(relayed & is_end)
        def _():
            drain(inbox.at[ch, 0], fresh_send)

        @pl.when(relayed & jnp.logical_not(is_end))
        def _():
            drain(inbox.at[ch, pl.ds(0, layers + 1)], fresh_send)

        return carry

    lax.fori_loop(0, chunks, finish, 0)
    drain(next_out.at[:, :, pl.ds(0, plane - 1)], out_send)
    drain(next_out.at[:, :, pl.ds(0, plane - 1)], out_recv)


def put(*refs):
    half = len(refs) // 2
    sems = refs[-1]
    copies = [
        pltpu.make_async_copy(refs[i], refs[half + i], sems.at[i]) for i in range(half)
    ]
    for copy in copies:
        copy.start()
    for copy in copies:
        copy.wait()


def settle(*arrays):
    return pl.pallas_call(
        put,
        out_shape=tuple(jax.ShapeDtypeStruct(a.shape, a.dtype) for a in arrays),
        in_specs=[pl.BlockSpec(memory_space=pltpu.VMEM)] * len(arrays),
        out_specs=(pl.BlockSpec(memory_space=pl.ANY),) * len(arrays),
        scratch_shapes=[pltpu.SemaphoreType.DMA((len(arrays),))],
        compiler_params=pltpu.CompilerParams(vmem_limit_bytes=1024 * 1024),
    )(*arrays)


def local(
    pool_tokens,
    cotangent,
    slot_weights,
    row_index,
    route_weight,
    slot_expert,
    next_expert,
    master,
    moment_m,
    moment_v,
):
    narrow_count = lax.axis_size("narrow")
    members = lax.axis_size("wide") * narrow_count
    parts, width, hidden_units = slot_weights.shape[1:]
    experts = master.shape[0]
    block = width // members
    length = row_index.shape[1]
    pool_count = pool_tokens.shape[0]
    plane = members // LAYERS
    cols = CHUNK_COLS
    split = min(SPLIT, max(1, block // ROW_TILE))
    piece = block // split
    chunks = parts * (hidden_units // cols) * split
    anywhere = pl.BlockSpec(memory_space=pl.ANY)
    scalars = pl.BlockSpec(memory_space=pltpu.SMEM)
    dma = pltpu.SemaphoreType.DMA
    bf16 = jnp.bfloat16
    state = pltpu.VMEM(master.shape, jnp.float32)
    held = pl.BlockSpec(memory_space=pltpu.VMEM)
    fresh, first, second, refilled, token_grads = pl.pallas_call(
        functools.partial(exchange, narrow_count, members),
        out_shape=(
            state,
            state,
            state,
            pltpu.VMEM((parts, LAYERS, plane, block, hidden_units), bf16),
            pltpu.VMEM(pool_tokens.shape, bf16),
        ),
        in_specs=[scalars, scalars, held, held] + [anywhere] * 6,
        out_specs=(held,) * 5,
        scratch_shapes=[
            pltpu.SMEM((experts * plane,), jnp.float32),
            pltpu.VMEM((chunks, plane, LAYERS, piece, cols), bf16),
            pltpu.VMEM((2 * pool_count, width), bf16),
            pltpu.VMEM((length, width), bf16),
            pltpu.VMEM((length, hidden_units), bf16),
            pltpu.VMEM((parts - 1, length, hidden_units), bf16),
            pltpu.VMEM((pool_count, length), bf16),
            pltpu.VMEM((length, 128), jnp.float32),
            pltpu.VMEM((2, length, hidden_units), jnp.float32),
            pltpu.VMEM((parts, width, hidden_units), bf16),
            pltpu.VMEM((2, 2 * pool_count, hidden_units), bf16),
            pltpu.VMEM((chunks, plane, LAYERS, piece, cols), bf16),
            pltpu.VMEM((chunks, LAYERS + 1, experts, piece, cols), bf16),
            pltpu.VMEM((LAYERS, experts, piece, cols), bf16),
            dma((4 + hidden_units // (UNIT * cols),)),
            dma((3,)),
            dma((chunks,)),
            dma((chunks,)),
            dma((chunks,)),
            dma,
            dma((chunks, LAYERS + 1)),
            dma,
            dma((chunks, LAYERS)),
            dma,
            dma,
        ],
        compiler_params=pltpu.CompilerParams(
            collective_id=0, has_side_effects=True, vmem_limit_bytes=46 * 1024 * 1024
        ),
    )(
        slot_expert[:, 0],
        next_expert[:, 0],
        row_index,
        route_weight,
        pool_tokens,
        cotangent,
        slot_weights,
        master,
        moment_m,
        moment_v,
    )
    next_weights = refilled.reshape(1, parts, width, hidden_units)
    return settle(token_grads, fresh, first, second, next_weights)


def solution(mesh):
    in_specs = (
        P(("wide", "narrow"), None),
        P(("wide", "narrow"), None),
        P(("wide", "narrow"), None, None, None),
        P(("wide", "narrow"), None),
        P(("wide", "narrow"), None),
        P(),
        P(),
        P(None, None, ("wide", "narrow"), None),
        P(None, None, ("wide", "narrow"), None),
        P(None, None, ("wide", "narrow"), None),
    )
    out_specs = (
        P(("wide", "narrow"), None),
        P(None, None, ("wide", "narrow"), None),
        P(None, None, ("wide", "narrow"), None),
        P(None, None, ("wide", "narrow"), None),
        P(("wide", "narrow"), None, None, None),
    )
    return jax.shard_map(local, mesh=mesh, in_specs=in_specs, out_specs=out_specs, check_vma=False)
```
